32 devices in a mesh: sub: 8 (over y, x, core), dir: 4 (over z).
Axes of the slice: x: 2, y: 2, z: 4, core: 2. Of those that a mesh axis runs over, the one named last changes fastest.
Arguments:
- fine_fields: float32 [8192, 2, 1024], P(('sub', 'dir')), may hold values from -6 to 6
- fine_octant: int32 [8192], P(('sub', 'dir')), may hold values from 0 to 7, as said below
- mid_octant: int32 [1024], P('sub'), may hold values from 0 to 7, as said below
- shift_fine: float32 [8, 4096], replicated, may hold values from -3.140625 to 3.140625
- shift_mid: float32 [8, 16384], replicated, may hold values from -3.140625 to 3.140625
- interp_theta_mid: float32 [64, 32], replicated, may hold values from -1 to 1
- interp_phi_mid: float32 [64, 32], replicated, may hold values from -1 to 1
- interp_theta_top: float32 [128, 64], replicated, may hold values from -0.75 to 0.75
- interp_phi_top: float32 [128, 64], replicated, may hold values from -0.75 to 0.75
- partners: int32 [128, 32], P('sub'), may hold values from 0 to 127, as said below
- translation: float32 [128, 32, 2, 16384], P('sub', None, None, 'dir'), may hold values from -0.0234375 to 0.0234375
Outputs:
- fine_incoming: float32 [8192, 2, 1024], P(('sub', 'dir'))
The draws below stay inside these ranges and needn't reach their ends.
Inputs may be any that keep to these rules, and one draw needn't show every extreme that they name: `fine_octant`: each aligned group of 8 entries is a permutation of 0 to 7. `mid_octant`: each aligned group of 8 entries is a permutation of 0 to 7. `partners`: row t names 32 different top boxes, none of them t.
All inputs are finite; a program needn't handle non-finite values.
Results may differ from the reference program's by a relative error of at most 0.000096.
Values sent between devices are 32-bit elements; how exact they have to be, the bound alone decides.
A program may use at most 128 MiB of HBM per device.

```python
import jax
import jax.numpy as jnp
from jax import lax

THETA_FINE = 32
PHI_FINE = 32
THETA_MID = 64
PHI_MID = 64
THETA_TOP = 128
PHI_TOP = 128
PARTNERS = 32
TOP = 128
MID = 1024
FINE = 8192
DIRS_FINE = 1024
DIRS_MID = 4096
DIRS_TOP = 16384


def octant_perm(key, groups):
    scores = jax.random.randint(key, (groups, 8), 0, 2 ** 20) * 8 + jnp.arange(8, dtype=jnp.int32)[None, :]
    return jnp.argsort(scores, axis=1, stable=True).astype(jnp.int32).reshape(-1)


def draw_fine_octant(key, part):
    return octant_perm(jax.random.fold_in(key, 11), MID)


def draw_mid_octant(key, part):
    return octant_perm(jax.random.fold_in(key, 12), TOP)


def draw_partners(key, part):
    scores = jax.random.randint(jax.random.fold_in(key, 13), (TOP, TOP), 0, 2 ** 16) * TOP
    scores = scores + jnp.arange(TOP, dtype=jnp.int32)[None, :]
    diagonal_mask = jnp.arange(TOP)[:, None] == jnp.arange(TOP)[None, :]
    scores = jnp.where(diagonal_mask, 2 ** 30, scores)
    return jnp.argsort(scores, axis=1, stable=True)[:, :PARTNERS].astype(jnp.int32)


def shard_levels(key, shape, pieces, low, high):
    factor_of, own = 1.0, jax.random.fold_in(key, 6)
    for dim, parts in pieces:
        draws = jnp.exp(jax.random.uniform(jax.random.fold_in(own, dim), (parts,), jnp.float32, low / len(pieces), high / len(pieces)))
        factor_of = factor_of * jnp.repeat(draws, shape[dim] // parts).reshape([-1 if axis == dim else 1 for axis in range(len(shape))])
    return factor_of


def normal_values(stream_key, shape, scale, reach, cuts=(), held_as=jnp.bfloat16):
    gain = shard_levels(stream_key, shape, cuts, -0.22, 0.18) if cuts else 1.0
    array = jax.random.normal(stream_key, shape, jnp.float32) * scale * gain
    return jnp.minimum(jnp.maximum(array, -reach), reach).astype(held_as)


def setup_inputs(seed: int = 0) -> dict:
    streams_of = jax.random.split(jax.random.key(seed), 12)
    return {
        "fine_fields": normal_values(streams_of[0], (FINE, 2, DIRS_FINE), 1.0, 6.0, ((0, 32),), jnp.float32),
        "fine_octant": draw_fine_octant(jax.random.fold_in(streams_of[11], 71), 0),
        "mid_octant": draw_mid_octant(jax.random.fold_in(streams_of[11], 71), 0),
        "shift_fine": jnp.clip(jax.random.uniform(streams_of[3], (8, DIRS_MID), jnp.float32, -3.140625, 3.140625), -3.140625, 3.140625),
        "shift_mid": jnp.clip(jax.random.uniform(streams_of[4], (8, DIRS_TOP), jnp.float32, -3.140625, 3.140625), -3.140625, 3.140625),
        "interp_theta_mid": normal_values(streams_of[5], (THETA_MID, THETA_FINE), THETA_FINE ** -0.5, 1.0, (), jnp.float32),
        "interp_phi_mid": normal_values(streams_of[6], (PHI_MID, PHI_FINE), PHI_FINE ** -0.5, 1.0, (), jnp.float32),
        "interp_theta_top": normal_values(streams_of[7], (THETA_TOP, THETA_MID), THETA_MID ** -0.5, 0.75, (), jnp.float32),
        "interp_phi_top": normal_values(streams_of[8], (PHI_TOP, PHI_MID), PHI_MID ** -0.5, 0.75, (), jnp.float32),
        "partners": draw_partners(jax.random.fold_in(streams_of[11], 71), 0),
        "translation": normal_values(streams_of[10], (TOP, PARTNERS, 2, DIRS_TOP), (1.0 / (8 * PARTNERS)), 0.0234375, ((0, 8), (3, 4)), jnp.float32),
    }


def interpolate(fields, theta_matrix, phi_matrix, theta_count, phi_count):
    boxes = fields.shape[0]
    grid = fields.reshape(boxes, 2, theta_count, phi_count)
    result = jnp.einsum("ta,bcap,fp->bctf", theta_matrix, grid, phi_matrix, precision=lax.Precision.HIGHEST)
    return result.reshape(boxes, 2, -1)


def anterpolate(fields, theta_matrix, phi_matrix):
    boxes = fields.shape[0]
    grid = fields.reshape(boxes, 2, theta_matrix.shape[0], phi_matrix.shape[0])
    result = jnp.einsum("ta,bctf,fp->bcap", theta_matrix, grid, phi_matrix, precision=lax.Precision.HIGHEST)
    return result.reshape(boxes, 2, -1)


def rotate(fields, angles, orient):
    cosine = jnp.cos(angles)
    sine = orient * jnp.sin(angles)
    real_part = fields[:, 0] * cosine - fields[:, 1] * sine
    imag_part = fields[:, 0] * sine + fields[:, 1] * cosine
    return jnp.stack([real_part, imag_part], axis=1)


def reference(fine_fields, fine_octant, mid_octant, shift_fine, shift_mid, interp_theta_mid, interp_phi_mid, interp_theta_top, interp_phi_top, partners, translation):
    fine_angles = shift_fine[fine_octant]
    mid_angles = shift_mid[mid_octant]
    child_mid = rotate(interpolate(fine_fields, interp_theta_mid, interp_phi_mid, THETA_FINE, PHI_FINE), fine_angles, 1.0)
    mid_fields = child_mid.reshape(MID, 8, 2, DIRS_MID).sum(axis=1)
    child_top = rotate(interpolate(mid_fields, interp_theta_top, interp_phi_top, THETA_MID, PHI_MID), mid_angles, 1.0)
    top_fields = child_top.reshape(TOP, 8, 2, DIRS_TOP).sum(axis=1)

    def one_box(inputs):
        listed, operator = inputs
        picked = top_fields[listed]
        real_part = picked[:, 0] * operator[:, 0] - picked[:, 1] * operator[:, 1]
        imag_part = picked[:, 0] * operator[:, 1] + picked[:, 1] * operator[:, 0]
        return jnp.stack([real_part.sum(axis=0), imag_part.sum(axis=0)], axis=0)

    top_incoming = lax.map(one_box, (partners, translation))
    parent_top = jnp.repeat(top_incoming, 8, axis=0)
    mid_incoming = anterpolate(rotate(parent_top, mid_angles, -1.0), interp_theta_top, interp_phi_top)
    parent_mid = jnp.repeat(mid_incoming, 8, axis=0)
    return anterpolate(rotate(parent_mid, fine_angles, -1.0), interp_theta_mid, interp_phi_mid)
```

```python
import functools

import jax
import jax.numpy as jnp
from jax import lax
from jax.experimental import pallas as pl
from jax.experimental.pallas import tpu as pltpu
from jax.sharding import PartitionSpec as P

LANES = 128
BF = jnp.bfloat16
F32 = jnp.float32


def split(x):
    hi = x.astype(BF)
    return hi, (x - hi.astype(F32)).astype(BF)


def mm(a, b):
    return jnp.dot(a, b, preferred_element_type=F32)


def wide_dot(x, w_hi, w_lo):
    hi, lo = split(x)
    return mm(hi, w_hi) + (mm(hi, w_lo) + mm(lo, w_hi))


def left3(a):
    hi, lo = split(a)
    return jnp.concatenate([hi, lo, hi], axis=1)


def right3(x):
    hi, lo = split(x)
    return jnp.concatenate([hi, hi, lo], axis=0)


def chunk_of(rows):
    return min(rows, 512)


def up_kernel(fine_oct, mid_oct, x_ref, wf_ref, af_ref, wt_ref, at_ref, cf_ref, sf_ref, ct_ref, st_ref,
              out_ref, y_ref, mid_ref, z_ref):
    pack = y_ref.shape[0]
    rows = y_ref.shape[1]
    theta_mid = cf_ref.shape[1]
    theta_fine = af_ref.shape[1]
    per = theta_fine // pack
    theta_top = ct_ref.shape[1]
    mids = mid_ref.shape[0] // theta_mid
    dirs, slots, _, band, _ = out_ref.shape
    half = LANES // 2

    wf_hi, wf_lo = split(wf_ref[...])
    step = chunk_of(rows)

    @pl.loop(0, rows // step)
    def _(i):
        base = pl.multiple_of(i * step, 8)
        re = x_ref[pl.ds(2 * base, step, stride=2), :]
        im = x_ref[pl.ds(2 * base + 1, step, stride=2), :]
        y = wide_dot(jnp.concatenate([re, im], axis=1), wf_hi, wf_lo)
        for a in range(pack):
            y_ref[a, pl.ds(base, step), :] = y[:, a * LANES:(a + 1) * LANES]

    a_mid = left3(af_ref[...])

    def box(b):
        start = pl.multiple_of(b * per, per)
        return jnp.concatenate([y_ref[a, pl.ds(start, per), :] for a in range(pack)], axis=0)

    def mid_step(m, carry):
        acc1 = jnp.zeros((theta_mid, LANES), F32)
        acc2 = jnp.zeros((theta_mid, LANES), F32)
        for i in range(0, 8, 2):
            b = m * 8 + i
            z = mm(a_mid, right3(jnp.concatenate([box(b), box(b + 1)], axis=1)))
            for side in range(2):
                o = fine_oct[b + side]
                part = z[:, side * LANES:(side + 1) * LANES]
                acc1 += part * cf_ref[o]
                acc2 += part * sf_ref[o]
        mid_ref[pl.ds(pl.multiple_of(m * theta_mid, theta_mid), theta_mid), :] = acc1 + pltpu.roll(acc2, half, 1)
        return carry

    lax.fori_loop(0, mids, mid_step, 0, unroll=2)

    wt_hi, wt_lo = split(wt_ref[...])
    mid_rows = mids * theta_mid
    step2 = chunk_of(mid_rows)

    @pl.loop(0, mid_rows // step2)
    def _(i):
        base = pl.multiple_of(i * step2, 8)
        z_ref[pl.ds(base, step2), :] = wide_dot(mid_ref[pl.ds(base, step2), :], wt_hi, wt_lo)

    a_top = left3(at_ref[...])
    out_ref[...] = jnp.zeros_like(out_ref)

    def top_step(m, carry):
        q = m // 8
        o = mid_oct[m]
        z = mm(a_top, right3(z_ref[pl.ds(pl.multiple_of(m * theta_mid, theta_mid), theta_mid), :]))
        for d in range(dirs):
            at = slice(d * band, (d + 1) * band)
            c, s = ct_ref[o, at, :], st_ref[o, at, :]
            re, im = z[at, :LANES], z[at, LANES:]
            out_ref[d, q, 0] += re * c - im * s
            out_ref[d, q, 1] += re * s + im * c
        return carry

    lax.fori_loop(0, mids, top_step, 0, unroll=2)


def down_kernel(fine_oct, mid_oct, r_ref, wf_ref, af_ref, wt_ref, at_ref, cf_ref, sf_ref, ct_ref, st_ref,
                out_ref, z_ref, mid_ref, y_ref):
    pack = y_ref.shape[0]
    rows = y_ref.shape[1]
    theta_mid = cf_ref.shape[1]
    theta_fine = af_ref.shape[0]
    per = theta_fine // pack
    mids = mid_ref.shape[0] // theta_mid
    dirs = r_ref.shape[0]
    half = LANES // 2

    a_hi, a_lo = split(at_ref[...])
    a_top = jnp.concatenate(
        [jnp.concatenate([a_hi, a_hi], axis=1), jnp.concatenate([a_lo, a_lo], axis=1)], axis=0)

    def top_step(m, carry):
        q = m // 8
        o = mid_oct[m]
        c, s = ct_ref[o], st_ref[o]
        re = jnp.concatenate([r_ref[d, q, 0] for d in range(dirs)], axis=0)
        im = jnp.concatenate([r_ref[d, q, 1] for d in range(dirs)], axis=0)
        hi, lo = split(jnp.concatenate([re * c + im * s, im * c - re * s], axis=1))
        z = mm(a_top, jnp.concatenate([hi, lo], axis=0))
        z_ref[pl.ds(pl.multiple_of(m * theta_mid, theta_mid), theta_mid), :] = z[:theta_mid] + z[theta_mid:]
        return carry

    lax.fori_loop(0, mids, top_step, 0, unroll=2)

    wt_hi, wt_lo = split(wt_ref[...])
    mid_rows = mids * theta_mid
    step2 = chunk_of(mid_rows)

    @pl.loop(0, mid_rows // step2)
    def _(i):
        base = pl.multiple_of(i * step2, 8)
        mid_ref[pl.ds(base, step2), :] = wide_dot(z_ref[pl.ds(base, step2), :], wt_hi, wt_lo)

    a_mid = left3(af_ref[...])

    def mid_step(m, carry):
        v = mid_ref[pl.ds(pl.multiple_of(m * theta_mid, theta_mid), theta_mid), :]
        turned = pltpu.roll(v, half, 1)
        for i in range(0, 8, 2):
            b = m * 8 + i
            both = []
            for side in range(2):
                o = fine_oct[b + side]
                both.append(v * cf_ref[o] + turned * sf_ref[o])
            z = mm(a_mid, right3(jnp.concatenate(both, axis=1)))
            for side in range(2):
                start = pl.multiple_of((b + side) * per, per)
                for a in range(pack):
                    y_ref[a, pl.ds(start, per), :] = z[a * per:(a + 1) * per, side * LANES:(side + 1) * LANES]
        return carry

    lax.fori_loop(0, mids, mid_step, 0, unroll=2)

    wf_hi, wf_lo = split(wf_ref[...])
    step = chunk_of(rows)

    @pl.loop(0, rows // step)
    def _(i):
        base = pl.multiple_of(i * step, 8)
        v = jnp.concatenate([y_ref[a, pl.ds(base, step), :] for a in range(pack)], axis=1)
        y = wide_dot(v, wf_hi, wf_lo)
        out_ref[pl.ds(2 * base, step, stride=2), :] = y[:, :LANES]
        out_ref[pl.ds(2 * base + 1, step, stride=2), :] = y[:, LANES:]


def translate_kernel(partners, p_ref, w_ref, out_ref):
    t = pl.program_id(0)
    band = p_ref.shape[2]

    def step(k, carry):
        re, im = carry
        n = partners[t, k]
        wr = w_ref[0, k, pl.ds(0, band, stride=2), :]
        wi = w_ref[0, k, pl.ds(1, band, stride=2), :]
        vr, vi = p_ref[n, 0], p_ref[n, 1]
        return re + (vr * wr - vi * wi), im + (vr * wi + vi * wr)

    zero = jnp.zeros((band, LANES), F32)
    re, im = lax.fori_loop(0, w_ref.shape[1], step, (zero, zero), unroll=4)
    out_ref[0, 0] = re
    out_ref[0, 1] = im


VM = pl.BlockSpec(memory_space=pltpu.VMEM)
SM = pl.BlockSpec(memory_space=pltpu.SMEM)


def body(fine_fields, fine_octant, mid_octant, shift_fine, shift_mid, interp_theta_mid, interp_phi_mid,
         interp_theta_top, interp_phi_top, partners, translation):
    theta_mid, theta_fine = interp_theta_mid.shape
    phi_mid, phi_fine = interp_phi_mid.shape
    theta_top, _ = interp_theta_top.shape
    phi_top, _ = interp_phi_top.shape
    dirs = lax.axis_size("dir")
    boxes = fine_fields.shape[0]
    mids = boxes // 8
    slots = mids // 8
    tops, listed, _, local = translation.shape
    band = local // phi_top
    pack = LANES // phi_fine
    per = theta_fine // pack
    rows = boxes * per

    mid_oct = lax.dynamic_slice_in_dim(mid_octant, lax.axis_index("dir") * mids, mids)
    x = fine_fields.reshape(boxes, 2, per, LANES).transpose(0, 2, 1, 3).reshape(rows * 2, LANES)
    w = translation.reshape(tops, listed, 2, band, LANES).transpose(0, 1, 3, 2, 4).reshape(
        tops, listed, 2 * band, LANES)

    cos_f = jnp.cos(shift_fine).reshape(8, theta_mid, phi_mid)
    sin_f = jnp.sin(shift_fine).reshape(8, theta_mid, phi_mid)
    cf = jnp.concatenate([cos_f, cos_f], axis=2)
    sf = jnp.concatenate([sin_f, -sin_f], axis=2)
    ct = jnp.cos(shift_mid).reshape(8, theta_top, phi_top)
    st = jnp.sin(shift_mid).reshape(8, theta_top, phi_top)

    two = jnp.eye(2, dtype=F32)
    lots = jnp.eye(pack, dtype=F32)
    wf = (two[:, None, None, None, :, None] * lots[None, :, None, :, None, None]
          * interp_phi_mid.T[None, None, :, None, None, :]).reshape(2 * LANES, pack * 2 * phi_mid)
    af = interp_theta_mid.reshape(theta_mid, per, pack).transpose(0, 2, 1).reshape(theta_mid, theta_fine)
    wt = (two[:, None, :, None] * interp_phi_top.T[None, :, None, :]).reshape(2 * phi_mid, 2 * phi_top)
    at = interp_theta_top

    params = pltpu.CompilerParams(vmem_limit_bytes=48 * 2**20)
    banded = pl.pallas_call(
        up_kernel,
        out_shape=jax.ShapeDtypeStruct((dirs, slots, 2, band, LANES), F32),
        in_specs=[SM, SM] + [VM] * 9,
        out_specs=VM,
        scratch_shapes=[
            pltpu.VMEM((pack, rows, LANES), F32),
            pltpu.VMEM((mids * theta_mid, LANES), F32),
            pltpu.VMEM((mids * theta_mid, 2 * LANES), F32),
        ],
        compiler_params=params,
        name="up",
    )(fine_octant, mid_oct, x, wf, af, wt, at, cf, sf, ct, st)

    received = lax.all_to_all(banded, "dir", split_axis=0, concat_axis=0, tiled=True)
    top_fields = received.reshape(tops, 2, band, LANES)
    portion = lax.all_gather(top_fields, "sub", axis=0, tiled=True)

    top_incoming = pl.pallas_call(
        translate_kernel,
        out_shape=jax.ShapeDtypeStruct((tops, 2, band, LANES), F32),
        grid=(tops,),
        in_specs=[
            SM,
            VM,
            pl.BlockSpec((1, listed, 2 * band, LANES), lambda t: (t, 0, 0, 0)),
        ],
        out_specs=pl.BlockSpec((1, 2, band, LANES), lambda t: (t, 0, 0, 0)),
        compiler_params=params,
        name="translate",
    )(partners, portion, w)

    parent = lax.all_to_all(
        top_incoming.reshape(dirs, slots, 2, band, LANES), "dir", split_axis=0, concat_axis=0, tiled=True)

    result = pl.pallas_call(
        down_kernel,
        out_shape=jax.ShapeDtypeStruct((rows * 2, LANES), F32),
        in_specs=[SM, SM] + [VM] * 9,
        out_specs=VM,
        scratch_shapes=[
            pltpu.VMEM((mids * theta_mid, 2 * LANES), F32),
            pltpu.VMEM((mids * theta_mid, LANES), F32),
            pltpu.VMEM((pack, rows, LANES), F32),
        ],
        compiler_params=params,
        name="down",
    )(fine_octant, mid_oct, parent, wf.T, af.T, wt.T, at.T, cf, sf, ct, st)
    return result.reshape(boxes, per, 2, LANES).transpose(0, 2, 1, 3).reshape(boxes, 2, theta_fine * phi_fine)


def solution(mesh):
    in_specs = (
        P(("sub", "dir"), None, None),
        P(("sub", "dir")),
        P("sub"),
        P(),
        P(),
        P(),
        P(),
        P(),
        P(),
        P("sub", None),
        P("sub", None, None, "dir"),
    )
    out_specs = P(("sub", "dir"), None, None)
    return jax.shard_map(body, mesh=mesh, in_specs=in_specs, out_specs=out_specs, check_vma=False)
```

```python
import jax
import jax.numpy as jnp
from jax import lax
from jax.experimental import pallas as pl
from jax.experimental.pallas import tpu as pltpu
from jax.sharding import PartitionSpec as P

LANES = 128
PIECES = 4
MESH = pl.DeviceIdType.MESH
BF = jnp.bfloat16
F32 = jnp.float32


def split(x):
    hi = x.astype(BF)
    return hi, (x - hi.astype(F32)).astype(BF)


def mm(a, b):
    return jnp.dot(a, b, preferred_element_type=F32)


def wide_dot(x, w_hi, w_lo):
    hi, lo = split(x)
    return mm(hi, w_hi) + (mm(hi, w_lo) + mm(lo, w_hi))


def left3(a):
    hi, lo = split(a)
    return jnp.concatenate([hi, lo, hi], axis=1)


def right3(x):
    hi, lo = split(x)
    return jnp.concatenate([hi, hi, lo], axis=0)


def chunk_of(rows):
    return min(rows, 512)


def up_kernel(fine_oct, mid_oct, x_ref, wf_ref, af_ref, wt_ref, at_ref, cf_ref, sf_ref, ct_ref, st_ref,
              out_ref, y_ref, mid_ref, z_ref):
    pack = y_ref.shape[0]
    rows = y_ref.shape[1]
    theta_mid = cf_ref.shape[1]
    theta_fine = af_ref.shape[1]
    per = theta_fine // pack
    theta_top = ct_ref.shape[1]
    mids = mid_ref.shape[0] // theta_mid
    dirs, slots, _, band, _ = out_ref.shape
    half = LANES // 2

    wf_hi, wf_lo = split(wf_ref[...])
    step = chunk_of(rows)

    @pl.loop(0, rows // step)
    def _(i):
        base = pl.multiple_of(i * step, 8)
        re = x_ref[pl.ds(2 * base, step, stride=2), :]
        im = x_ref[pl.ds(2 * base + 1, step, stride=2), :]
        y = wide_dot(jnp.concatenate([re, im], axis=1), wf_hi, wf_lo)
        for a in range(pack):
            y_ref[a, pl.ds(base, step), :] = y[:, a * LANES:(a + 1) * LANES]

    a_mid = left3(af_ref[...])

    def box(b):
        start = pl.multiple_of(b * per, per)
        return jnp.concatenate([y_ref[a, pl.ds(start, per), :] for a in range(pack)], axis=0)

    def mid_step(m, carry):
        acc1 = jnp.zeros((theta_mid, LANES), F32)
        acc2 = jnp.zeros((theta_mid, LANES), F32)
        for i in range(0, 8, 2):
            b = m * 8 + i
            z = mm(a_mid, right3(jnp.concatenate([box(b), box(b + 1)], axis=1)))
            for side in range(2):
                o = fine_oct[b + side]
                part = z[:, side * LANES:(side + 1) * LANES]
                acc1 += part * cf_ref[o]
                acc2 += part * sf_ref[o]
        mid_ref[pl.ds(pl.multiple_of(m * theta_mid, theta_mid), theta_mid), :] = acc1 + pltpu.roll(acc2, half, 1)
        return carry

    lax.fori_loop(0, mids, mid_step, 0, unroll=2)

    wt_hi, wt_lo = split(wt_ref[...])
    mid_rows = mids * theta_mid
    step2 = chunk_of(mid_rows)

    @pl.loop(0, mid_rows // step2)
    def _(i):
        base = pl.multiple_of(i * step2, 8)
        z_ref[pl.ds(base, step2), :] = wide_dot(mid_ref[pl.ds(base, step2), :], wt_hi, wt_lo)

    a_top = left3(at_ref[...])
    out_ref[...] = jnp.zeros_like(out_ref)

    def top_step(m, carry):
        q = m // 8
        o = mid_oct[m]
        z = mm(a_top, right3(z_ref[pl.ds(pl.multiple_of(m * theta_mid, theta_mid), theta_mid), :]))
        for d in range(dirs):
            at = slice(d * band, (d + 1) * band)
            c, s = ct_ref[o, at, :], st_ref[o, at, :]
            re, im = z[at, :LANES], z[at, LANES:]
            out_ref[d, q, 0] += re * c - im * s
            out_ref[d, q, 1] += re * s + im * c
        return carry

    lax.fori_loop(0, mids, top_step, 0, unroll=2)


def down_kernel(fine_oct, mid_oct, r_ref, wf_ref, af_ref, wt_ref, at_ref, cf_ref, sf_ref, ct_ref, st_ref,
                out_ref, z_ref, mid_ref, y_ref):
    pack = y_ref.shape[0]
    rows = y_ref.shape[1]
    theta_mid = cf_ref.shape[1]
    theta_fine = af_ref.shape[0]
    per = theta_fine // pack
    mids = mid_ref.shape[0] // theta_mid
    dirs = r_ref.shape[0]
    half = LANES // 2

    a_hi, a_lo = split(at_ref[...])
    a_top = jnp.concatenate(
        [jnp.concatenate([a_hi, a_hi], axis=1), jnp.concatenate([a_lo, a_lo], axis=1)], axis=0)

    def top_step(m, carry):
        q = m // 8
        o = mid_oct[m]
        c, s = ct_ref[o], st_ref[o]
        re = jnp.concatenate([r_ref[d, q, 0] for d in range(dirs)], axis=0)
        im = jnp.concatenate([r_ref[d, q, 1] for d in range(dirs)], axis=0)
        hi, lo = split(jnp.concatenate([re * c + im * s, im * c - re * s], axis=1))
        z = mm(a_top, jnp.concatenate([hi, lo], axis=0))
        z_ref[pl.ds(pl.multiple_of(m * theta_mid, theta_mid), theta_mid), :] = z[:theta_mid] + z[theta_mid:]
        return carry

    lax.fori_loop(0, mids, top_step, 0, unroll=2)

    wt_hi, wt_lo = split(wt_ref[...])
    mid_rows = mids * theta_mid
    step2 = chunk_of(mid_rows)

    @pl.loop(0, mid_rows // step2)
    def _(i):
        base = pl.multiple_of(i * step2, 8)
        mid_ref[pl.ds(base, step2), :] = wide_dot(z_ref[pl.ds(base, step2), :], wt_hi, wt_lo)

    a_mid = left3(af_ref[...])

    def mid_step(m, carry):
        v = mid_ref[pl.ds(pl.multiple_of(m * theta_mid, theta_mid), theta_mid), :]
        turned = pltpu.roll(v, half, 1)
        for i in range(0, 8, 2):
            b = m * 8 + i
            both = []
            for side in range(2):
                o = fine_oct[b + side]
                both.append(v * cf_ref[o] + turned * sf_ref[o])
            z = mm(a_mid, right3(jnp.concatenate(both, axis=1)))
            for side in range(2):
                start = pl.multiple_of((b + side) * per, per)
                for a in range(pack):
                    y_ref[a, pl.ds(start, per), :] = z[a * per:(a + 1) * per, side * LANES:(side + 1) * LANES]
        return carry

    lax.fori_loop(0, mids, mid_step, 0, unroll=2)

    wf_hi, wf_lo = split(wf_ref[...])
    step = chunk_of(rows)

    @pl.loop(0, rows // step)
    def _(i):
        base = pl.multiple_of(i * step, 8)
        v = jnp.concatenate([y_ref[a, pl.ds(base, step), :] for a in range(pack)], axis=1)
        y = wide_dot(v, wf_hi, wf_lo)
        out_ref[pl.ds(2 * base, step, stride=2), :] = y[:, :LANES]
        out_ref[pl.ds(2 * base + 1, step, stride=2), :] = y[:, LANES:]


def exchange_kernel(partners, banded_ref, w_hbm, out_ref, p_ref, w_ref, o_ref,
                    w_sem, own_sem, a_send, a_recv, cw_send, cw_recv, ccw_send, ccw_recv,
                    part_send, part_recv, r_send, r_recv):
    dirs, slots, _, band, _ = banded_ref.shape
    tops, listed = w_ref.shape[:2]
    subs = p_ref.shape[0] // tops
    chips = subs // 2
    wide = chips // 2
    hops = chips // 2
    group = dirs // PIECES
    many = group * slots

    me = lax.axis_index("sub")
    z = lax.axis_index("dir")
    core = lax.rem(me, 2)

    def flip(c):
        return jnp.where(c < wide, c, 3 * wide - 1 - c)

    ring = flip(me // 2)

    def at_ring(step):
        return 2 * flip(lax.rem(ring + step + chips, chips)) + core

    right, left = at_ring(1), at_ring(-1)
    partner = me + 1 - 2 * core
    peers = [lax.rem(z + e, dirs) for e in range(1, dirs)]

    barrier = pltpu.get_barrier_semaphore()
    for d in peers:
        pl.semaphore_signal(barrier, inc=1, device_id=(me, d), device_id_type=MESH)
    for s in (right, left, partner):
        pl.semaphore_signal(barrier, inc=1, device_id=(s, z), device_id_type=MESH)
    pl.semaphore_wait(barrier, dirs + 2)

    def push(src, dst, send, recv, device):
        return pltpu.make_async_remote_copy(
            src_ref=src, dst_ref=dst, send_sem=send, recv_sem=recv, device_id=device, device_id_type=MESH)

    def block(source):
        return p_ref.at[pl.ds(me * tops + source * slots, slots)]

    own = pltpu.make_async_copy(banded_ref.at[z], block(z), own_sem)
    own.start()
    first = []
    for e in range(1, dirs):
        d = lax.rem(z - e + dirs, dirs)
        copy = push(banded_ref.at[d], block(z), a_send.at[e], a_recv.at[e], (me, d))
        copy.start()
        first.append(copy)
    loads = []
    for t in range(tops):
        copy = pltpu.make_async_copy(w_hbm.at[t], w_ref.at[t], w_sem.at[t])
        copy.start()
        loads.append(copy)

    def piece(sub, i):
        g = lax.rem(z // group + i, PIECES)
        return p_ref.at[pl.ds(sub * tops + g * many, many)]

    sent, handed = [], []

    def ship(view, send, recv, device, keep):
        copy = push(view, view, send, recv, device)
        copy.start()
        keep.append(copy)

    own.wait()
    arrived = 0
    for step in range(PIECES + hops):
        if step < PIECES:
            last = dirs - 1 if step == PIECES - 1 or group > 1 else step
            while arrived < last:
                first[arrived].wait_recv()
                arrived += 1
            view = piece(me, step)
            ship(view, cw_send.at[0, step], cw_recv.at[0, step], (right, z), sent)
            ship(view, ccw_send.at[0, step], ccw_recv.at[0, step], (left, z), sent)
            ship(view, part_send.at[0, step], part_recv.at[0, step], (partner, z), handed)
        for h in range(1, hops + 1):
            i = step - h
            if not 0 <= i < PIECES:
                continue
            for way in range(2):
                forward = i < PIECES // 2 if way == 0 else i >= PIECES // 2
                if h == hops and not forward:
                    continue
                send, recv = (cw_send, cw_recv) if way == 0 else (ccw_send, ccw_recv)
                target = right if way == 0 else left
                view = piece(at_ring(-h if way == 0 else h), i)
                push(view, view, send.at[h - 1, i], recv.at[h - 1, i], (target, z)).wait_recv()
                if h + 1 < hops or (h + 1 == hops and forward):
                    ship(view, send.at[h, i], recv.at[h, i], (target, z), sent)
                slot = 2 * h - 1 + way
                ship(view, part_send.at[slot, i], part_recv.at[slot, i], (partner, z), handed)
    for copy in handed:
        copy.wait_recv()
    for copy in loads:
        copy.wait()

    def translate(t):
        def one(k, carry):
            re, im = carry
            n = partners[t, k]
            wr = w_ref[t, k, pl.ds(0, band, stride=2), :]
            wi = w_ref[t, k, pl.ds(1, band, stride=2), :]
            vr, vi = p_ref[n, 0], p_ref[n, 1]
            return re + (vr * wr - vi * wi), im + (vr * wi + vi * wr)

        zero = jnp.zeros((band, LANES), F32)
        re, im = lax.fori_loop(0, listed, one, (zero, zero), unroll=4)
        o_ref[t, 0] = re
        o_ref[t, 1] = im

    returns = []
    waiting = None
    for e in range(1, dirs + 1):
        d = lax.rem(z + e, dirs)
        translate(d * slots)
        if waiting is not None:
            waiting.start()
            returns.append(waiting)
            waiting = None
        if slots > 1:
            def more(q, carry, d=d):
                translate(d * slots + q)
                return carry

            lax.fori_loop(1, slots, more, 0)
        if e < dirs:
            waiting = push(o_ref.at[pl.ds(d * slots, slots)], out_ref.at[z], r_send.at[e], r_recv.at[e], (me, d))
    for copy in returns:
        copy.wait()
    own = pltpu.make_async_copy(o_ref.at[pl.ds(z * slots, slots)], out_ref.at[z], own_sem)
    own.start()
    for copy in first + sent + handed:
        copy.wait_send()
    own.wait()


VM = pl.BlockSpec(memory_space=pltpu.VMEM)
SM = pl.BlockSpec(memory_space=pltpu.SMEM)
ANY = pl.BlockSpec(memory_space=pl.ANY)


def body(fine_fields, fine_octant, mid_octant, shift_fine, shift_mid, interp_theta_mid, interp_phi_mid,
         interp_theta_top, interp_phi_top, partners, translation):
    theta_mid, theta_fine = interp_theta_mid.shape
    phi_mid, phi_fine = interp_phi_mid.shape
    theta_top, _ = interp_theta_top.shape
    phi_top, _ = interp_phi_top.shape
    dirs = lax.axis_size("dir")
    boxes = fine_fields.shape[0]
    mids = boxes // 8
    slots = mids // 8
    tops, listed, _, local = translation.shape
    band = local // phi_top
    pack = LANES // phi_fine
    per = theta_fine // pack
    rows = boxes * per

    mid_oct = lax.dynamic_slice_in_dim(mid_octant, lax.axis_index("dir") * mids, mids)
    x = fine_fields.reshape(boxes, 2, per, LANES).transpose(0, 2, 1, 3).reshape(rows * 2, LANES)
    w = translation.reshape(tops, listed, 2, band, LANES).transpose(0, 1, 3, 2, 4).reshape(
        tops, listed, 2 * band, LANES)

    cos_f = jnp.cos(shift_fine).reshape(8, theta_mid, phi_mid)
    sin_f = jnp.sin(shift_fine).reshape(8, theta_mid, phi_mid)
    cf = jnp.concatenate([cos_f, cos_f], axis=2)
    sf = jnp.concatenate([sin_f, -sin_f], axis=2)
    ct = jnp.cos(shift_mid).reshape(8, theta_top, phi_top)
    st = jnp.sin(shift_mid).reshape(8, theta_top, phi_top)

    two = jnp.eye(2, dtype=F32)
    lots = jnp.eye(pack, dtype=F32)
    wf = (two[:, None, None, None, :, None] * lots[None, :, None, :, None, None]
          * interp_phi_mid.T[None, None, :, None, None, :]).reshape(2 * LANES, pack * 2 * phi_mid)
    af = interp_theta_mid.reshape(theta_mid, per, pack).transpose(0, 2, 1).reshape(theta_mid, theta_fine)
    wt = (two[:, None, :, None] * interp_phi_top.T[None, :, None, :]).reshape(2 * phi_mid, 2 * phi_top)
    at = interp_theta_top

    params = pltpu.CompilerParams(vmem_limit_bytes=48 * 2**20)
    banded = pl.pallas_call(
        up_kernel,
        out_shape=jax.ShapeDtypeStruct((dirs, slots, 2, band, LANES), F32),
        in_specs=[SM, SM] + [VM] * 9,
        out_specs=VM,
        scratch_shapes=[
            pltpu.VMEM((pack, rows, LANES), F32),
            pltpu.VMEM((mids * theta_mid, LANES), F32),
            pltpu.VMEM((mids * theta_mid, 2 * LANES), F32),
        ],
        compiler_params=params,
        name="up",
    )(fine_octant, mid_oct, x, wf, af, wt, at, cf, sf, ct, st)

    subs = lax.axis_size("sub")
    hops = subs // 4
    dma = pltpu.SemaphoreType.DMA
    parent = pl.pallas_call(
        exchange_kernel,
        out_shape=jax.ShapeDtypeStruct((dirs, slots, 2, band, LANES), F32),
        in_specs=[SM, ANY, ANY],
        out_specs=ANY,
        scratch_shapes=[
            pltpu.VMEM((subs * tops, 2, band, LANES), F32),
            pltpu.VMEM((tops, listed, 2 * band, LANES), F32),
            pltpu.VMEM((tops, 2, band, LANES), F32),
            dma((tops,)),
            dma,
            dma((dirs,)),
            dma((dirs,)),
            dma((hops, PIECES)),
            dma((hops, PIECES)),
            dma((hops, PIECES)),
            dma((hops, PIECES)),
            dma((2 * hops + 1, PIECES)),
            dma((2 * hops + 1, PIECES)),
            dma((dirs,)),
            dma((dirs,)),
        ],
        compiler_params=pltpu.CompilerParams(
            vmem_limit_bytes=48 * 2**20, collective_id=0, has_side_effects=True),
        name="exchange",
    )(partners, banded, w)

    result = pl.pallas_call(
        down_kernel,
        out_shape=jax.ShapeDtypeStruct((rows * 2, LANES), F32),
        in_specs=[SM, SM] + [VM] * 9,
        out_specs=VM,
        scratch_shapes=[
            pltpu.VMEM((mids * theta_mid, 2 * LANES), F32),
            pltpu.VMEM((mids * theta_mid, LANES), F32),
            pltpu.VMEM((pack, rows, LANES), F32),
        ],
        compiler_params=params,
        name="down",
    )(fine_octant, mid_oct, parent, wf.T, af.T, wt.T, at.T, cf, sf, ct, st)
    return result.reshape(boxes, per, 2, LANES).transpose(0, 2, 1, 3).reshape(boxes, 2, theta_fine * phi_fine)


def solution(mesh):
    in_specs = (
        P(("sub", "dir"), None, None),
        P(("sub", "dir")),
        P("sub"),
        P(),
        P(),
        P(),
        P(),
        P(),
        P(),
        P("sub", None),
        P("sub", None, None, "dir"),
    )
    out_specs = P(("sub", "dir"), None, None)
    return jax.shard_map(body, mesh=mesh, in_specs=in_specs, out_specs=out_specs, check_vma=False)
```

```python
import jax
import jax.numpy as jnp
from jax import lax
from jax.experimental import pallas as pl
from jax.experimental.pallas import tpu as pltpu
from jax.sharding import PartitionSpec as P

LANES = 128
MESH = pl.DeviceIdType.MESH
BF = jnp.bfloat16
F32 = jnp.float32


def split(x):
    hi = x.astype(BF)
    return hi, (x - hi.astype(F32)).astype(BF)


def mm(a, b):
    return jnp.dot(a, b, preferred_element_type=F32)


def wide_dot(x, w_hi, w_lo):
    hi, lo = split(x)
    return mm(hi, w_hi) + (mm(hi, w_lo) + mm(lo, w_hi))


def left3(a):
    hi, lo = split(a)
    return jnp.concatenate([hi, lo, hi], axis=1)


def right3(x):
    hi, lo = split(x)
    return jnp.concatenate([hi, hi, lo], axis=0)


def chunk_of(rows):
    return min(rows, 512)


def up_kernel(fine_oct, mid_oct, partners, x_ref, wf_ref, af_ref, wt_ref, at_ref, cf_ref, sf_ref, ct_ref, st_ref,
              w_hbm, out_ref, y_ref, mid_ref, z_ref, banded_ref, p_ref, w_ref, o_ref,
              w_sem, own_sem, last_sem, a_send, a_recv, cw_send, cw_recv, ccw_send, ccw_recv,
              part_send, part_recv, r_send, r_recv):
    pack, step, _ = y_ref.shape
    theta_mid = cf_ref.shape[1]
    theta_fine = af_ref.shape[1]
    per = theta_fine // pack
    half = LANES // 2
    dirs, slots, _, band, _ = banded_ref.shape
    tops, listed = w_ref.shape[:2]
    subs = p_ref.shape[0] // tops
    chips = subs // 2
    wide = chips // 2
    hops = chips // 2

    me = lax.axis_index("sub")
    z = lax.axis_index("dir")
    core = lax.rem(me, 2)

    def flip(c):
        return jnp.where(c < wide, c, 3 * wide - 1 - c)

    ring = flip(me // 2)

    def at_ring(move):
        return 2 * flip(lax.rem(ring + move + chips, chips)) + core

    right, left = at_ring(1), at_ring(-1)
    partner = me + 1 - 2 * core

    barrier = pltpu.get_barrier_semaphore()
    for e in range(1, dirs):
        pl.semaphore_signal(barrier, inc=1, device_id=(me, lax.rem(z + e, dirs)), device_id_type=MESH)
    for s in (right, left, partner):
        pl.semaphore_signal(barrier, inc=1, device_id=(s, z), device_id_type=MESH)
    loads = []
    for t in range(tops):
        copy = pltpu.make_async_copy(w_hbm.at[t], w_ref.at[t], w_sem.at[t])
        copy.start()
        loads.append(copy)
    pl.semaphore_wait(barrier, dirs + 2)

    def push(src, dst, send, recv, device):
        return pltpu.make_async_remote_copy(
            src_ref=src, dst_ref=dst, send_sem=send, recv_sem=recv, device_id=device, device_id_type=MESH)

    def spread(q):
        dst = p_ref.at[me * tops + q * dirs + z]
        copies = []
        for e in range(1, dirs):
            d = lax.rem(z - e + dirs, dirs)
            copies.append(push(banded_ref.at[d, q], dst, a_send.at[e, q], a_recv.at[e, q], (me, d)))
        return copies, pltpu.make_async_copy(banded_ref.at[z, q], dst, own_sem.at[q])

    def start_spread(q):
        copies, own = spread(q)
        for copy in copies:
            copy.start()
        own.start()

    def piece(sub, i):
        return p_ref.at[pl.ds(sub * tops + i * dirs, dirs)]

    def own_copies(q):
        view = piece(me, q)
        return [
            push(view, view, cw_send.at[0, q], cw_recv.at[0, q], (right, z)),
            push(view, view, ccw_send.at[0, q], ccw_recv.at[0, q], (left, z)),
            push(view, view, part_send.at[0, q], part_recv.at[0, q], (partner, z)),
        ]

    def own_ship(q):
        copies, own = spread(q)
        for copy in copies:
            copy.wait_recv()
        own.wait()
        for copy in own_copies(q):
            copy.start()

    wf_hi, wf_lo = split(wf_ref[...])
    wt_hi, wt_lo = split(wt_ref[...])
    a_mid = left3(af_ref[...])
    a_top = left3(at_ref[...])
    banded_ref[...] = jnp.zeros_like(banded_ref)

    @pl.loop(0, slots)
    def _(q):
        base = pl.multiple_of(q * step, 8)
        re = x_ref[pl.ds(2 * base, step, stride=2), :]
        im = x_ref[pl.ds(2 * base + 1, step, stride=2), :]
        y = wide_dot(jnp.concatenate([re, im], axis=1), wf_hi, wf_lo)
        for a in range(pack):
            y_ref[a] = y[:, a * LANES:(a + 1) * LANES]

        @pl.when(q > 0)
        def _():
            start_spread(q - 1)

        @pl.when(q > 1)
        def _():
            own_ship(q - 2)

        def box(b):
            start = pl.multiple_of(b * per, per)
            return jnp.concatenate([y_ref[a, pl.ds(start, per), :] for a in range(pack)], axis=0)

        def mid_step(m, carry):
            acc1 = jnp.zeros((theta_mid, LANES), F32)
            acc2 = jnp.zeros((theta_mid, LANES), F32)
            for i in range(0, 8, 2):
                b = m * 8 + i
                v = mm(a_mid, right3(jnp.concatenate([box(b), box(b + 1)], axis=1)))
                for side in range(2):
                    o = fine_oct[q * 64 + b + side]
                    part = v[:, side * LANES:(side + 1) * LANES]
                    acc1 += part * cf_ref[o]
                    acc2 += part * sf_ref[o]
            mid_ref[pl.ds(pl.multiple_of(m * theta_mid, theta_mid), theta_mid), :] = acc1 + pltpu.roll(acc2, half, 1)
            return carry

        lax.fori_loop(0, 8, mid_step, 0, unroll=2)
        z_ref[...] = wide_dot(mid_ref[...], wt_hi, wt_lo)

        def top_step(m, carry):
            o = mid_oct[q * 8 + m]
            v = mm(a_top, right3(z_ref[pl.ds(pl.multiple_of(m * theta_mid, theta_mid), theta_mid), :]))
            for d in range(dirs):
                at = slice(d * band, (d + 1) * band)
                c, s = ct_ref[o, at, :], st_ref[o, at, :]
                re, im = v[at, :LANES], v[at, LANES:]
                banded_ref[d, q, 0] += re * c - im * s
                banded_ref[d, q, 1] += re * s + im * c
            return carry

        lax.fori_loop(0, 8, top_step, 0, unroll=2)

    if slots > 1:
        own_ship(slots - 2)
    start_spread(slots - 1)

    sent, handed = [], []

    def ship(view, send, recv, device, keep):
        copy = push(view, view, send, recv, device)
        copy.start()
        keep.append(copy)

    for turn in range(1, slots + hops):
        if turn == min(slots, 2):
            own_ship(slots - 1)
        for h in range(1, hops + 1):
            i = turn - h
            if not 0 <= i < slots:
                continue
            for way in range(2):
                forward = i < slots // 2 if way == 0 else i >= slots // 2
                if h == hops and not forward:
                    continue
                send, recv = (cw_send, cw_recv) if way == 0 else (ccw_send, ccw_recv)
                target = right if way == 0 else left
                view = piece(at_ring(-h if way == 0 else h), i)
                push(view, view, send.at[h - 1, i], recv.at[h - 1, i], (target, z)).wait_recv()
                if h + 1 < hops or (h + 1 == hops and forward):
                    ship(view, send.at[h, i], recv.at[h, i], (target, z), sent)
                slot = 2 * h - 1 + way
                ship(view, part_send.at[slot, i], part_recv.at[slot, i], (partner, z), handed)
    for q in range(slots):
        own_copies(q)[2].wait_recv()
    for copy in handed:
        copy.wait_recv()
    for copy in loads:
        copy.wait()

    def translate(t):
        def one(k, carry):
            re, im = carry
            n = partners[t, k]
            wr = w_ref[t, k, pl.ds(0, band, stride=2), :]
            wi = w_ref[t, k, pl.ds(1, band, stride=2), :]
            vr, vi = p_ref[n, 0], p_ref[n, 1]
            return re + (vr * wr - vi * wi), im + (vr * wi + vi * wr)

        zero = jnp.zeros((band, LANES), F32)
        re, im = lax.fori_loop(0, listed, one, (zero, zero), unroll=4)
        o_ref[t, 0] = re
        o_ref[t, 1] = im

    returns = []
    waiting = None
    for e in range(1, dirs + 1):
        d = lax.rem(z + e, dirs)
        translate(d * slots)
        if waiting is not None:
            waiting.start()
            returns.append(waiting)
            waiting = None
        if slots > 1:
            def more(q, carry, d=d):
                translate(d * slots + q)
                return carry

            lax.fori_loop(1, slots, more, 0)
        if e < dirs:
            waiting = push(o_ref.at[pl.ds(d * slots, slots)], out_ref.at[z], r_send.at[e], r_recv.at[e], (me, d))
    for copy in returns:
        copy.wait()
    own = pltpu.make_async_copy(o_ref.at[pl.ds(z * slots, slots)], out_ref.at[z], last_sem)
    own.start()
    for q in range(slots):
        for copy in spread(q)[0] + own_copies(q):
            copy.wait_send()
    for copy in sent + handed:
        copy.wait_send()
    own.wait()


def down_kernel(fine_oct, mid_oct, r_ref, wf_ref, af_ref, wt_ref, at_ref, cf_ref, sf_ref, ct_ref, st_ref,
                out_ref, z_ref, mid_ref, y_ref):
    pack = y_ref.shape[0]
    rows = y_ref.shape[1]
    theta_mid = cf_ref.shape[1]
    theta_fine = af_ref.shape[0]
    per = theta_fine // pack
    mids = mid_ref.shape[0] // theta_mid
    dirs = r_ref.shape[0]
    half = LANES // 2

    a_hi, a_lo = split(at_ref[...])
    a_top = jnp.concatenate(
        [jnp.concatenate([a_hi, a_hi], axis=1), jnp.concatenate([a_lo, a_lo], axis=1)], axis=0)

    def top_step(m, carry):
        q = m // 8
        o = mid_oct[m]
        c, s = ct_ref[o], st_ref[o]
        re = jnp.concatenate([r_ref[d, q, 0] for d in range(dirs)], axis=0)
        im = jnp.concatenate([r_ref[d, q, 1] for d in range(dirs)], axis=0)
        hi, lo = split(jnp.concatenate([re * c + im * s, im * c - re * s], axis=1))
        z = mm(a_top, jnp.concatenate([hi, lo], axis=0))
        z_ref[pl.ds(pl.multiple_of(m * theta_mid, theta_mid), theta_mid), :] = z[:theta_mid] + z[theta_mid:]
        return carry

    lax.fori_loop(0, mids, top_step, 0, unroll=2)

    wt_hi, wt_lo = split(wt_ref[...])
    mid_rows = mids * theta_mid
    step2 = chunk_of(mid_rows)

    @pl.loop(0, mid_rows // step2)
    def _(i):
        base = pl.multiple_of(i * step2, 8)
        mid_ref[pl.ds(base, step2), :] = wide_dot(z_ref[pl.ds(base, step2), :], wt_hi, wt_lo)

    a_mid = left3(af_ref[...])

    def mid_step(m, carry):
        v = mid_ref[pl.ds(pl.multiple_of(m * theta_mid, theta_mid), theta_mid), :]
        turned = pltpu.roll(v, half, 1)
        for i in range(0, 8, 2):
            b = m * 8 + i
            both = []
            for side in range(2):
                o = fine_oct[b + side]
                both.append(v * cf_ref[o] + turned * sf_ref[o])
            z = mm(a_mid, right3(jnp.concatenate(both, axis=1)))
            for side in range(2):
                start = pl.multiple_of((b + side) * per, per)
                for a in range(pack):
                    y_ref[a, pl.ds(start, per), :] = z[a * per:(a + 1) * per, side * LANES:(side + 1) * LANES]
        return carry

    lax.fori_loop(0, mids, mid_step, 0, unroll=2)

    wf_hi, wf_lo = split(wf_ref[...])
    step = chunk_of(rows)

    @pl.loop(0, rows // step)
    def _(i):
        base = pl.multiple_of(i * step, 8)
        v = jnp.concatenate([y_ref[a, pl.ds(base, step), :] for a in range(pack)], axis=1)
        y = wide_dot(v, wf_hi, wf_lo)
        out_ref[pl.ds(2 * base, step, stride=2), :] = y[:, :LANES]
        out_ref[pl.ds(2 * base + 1, step, stride=2), :] = y[:, LANES:]


VM = pl.BlockSpec(memory_space=pltpu.VMEM)
SM = pl.BlockSpec(memory_space=pltpu.SMEM)
ANY = pl.BlockSpec(memory_space=pl.ANY)


def body(fine_fields, fine_octant, mid_octant, shift_fine, shift_mid, interp_theta_mid, interp_phi_mid,
         interp_theta_top, interp_phi_top, partners, translation):
    theta_mid, theta_fine = interp_theta_mid.shape
    phi_mid, phi_fine = interp_phi_mid.shape
    theta_top, _ = interp_theta_top.shape
    phi_top, _ = interp_phi_top.shape
    dirs = lax.axis_size("dir")
    boxes = fine_fields.shape[0]
    mids = boxes // 8
    slots = mids // 8
    tops, listed, _, local = translation.shape
    band = local // phi_top
    pack = LANES // phi_fine
    per = theta_fine // pack
    rows = boxes * per

    mid_oct = lax.dynamic_slice_in_dim(mid_octant, lax.axis_index("dir") * mids, mids)
    x = fine_fields.reshape(boxes, 2, per, LANES).transpose(0, 2, 1, 3).reshape(rows * 2, LANES)
    w = translation.reshape(tops, listed, 2, band, LANES).transpose(0, 1, 3, 2, 4).reshape(
        tops, listed, 2 * band, LANES)

    cos_f = jnp.cos(shift_fine).reshape(8, theta_mid, phi_mid)
    sin_f = jnp.sin(shift_fine).reshape(8, theta_mid, phi_mid)
    cf = jnp.concatenate([cos_f, cos_f], axis=2)
    sf = jnp.concatenate([sin_f, -sin_f], axis=2)
    ct = jnp.cos(shift_mid).reshape(8, theta_top, phi_top)
    st = jnp.sin(shift_mid).reshape(8, theta_top, phi_top)

    two = jnp.eye(2, dtype=F32)
    lots = jnp.eye(pack, dtype=F32)
    wf = (two[:, None, None, None, :, None] * lots[None, :, None, :, None, None]
          * interp_phi_mid.T[None, None, :, None, None, :]).reshape(2 * LANES, pack * 2 * phi_mid)
    af = interp_theta_mid.reshape(theta_mid, per, pack).transpose(0, 2, 1).reshape(theta_mid, theta_fine)
    wt = (two[:, None, :, None] * interp_phi_top.T[None, :, None, :]).reshape(2 * phi_mid, 2 * phi_top)
    at = interp_theta_top

    params = pltpu.CompilerParams(vmem_limit_bytes=48 * 2**20)
    subs = lax.axis_size("sub")
    hops = subs // 4
    dma = pltpu.SemaphoreType.DMA
    inside = partners % tops
    place = partners - inside + inside % slots * dirs + inside // slots
    parent = pl.pallas_call(
        up_kernel,
        out_shape=jax.ShapeDtypeStruct((dirs, slots, 2, band, LANES), F32),
        in_specs=[SM] * 3 + [VM] * 9 + [ANY],
        out_specs=ANY,
        scratch_shapes=[
            pltpu.VMEM((pack, rows // slots, LANES), F32),
            pltpu.VMEM((8 * theta_mid, LANES), F32),
            pltpu.VMEM((8 * theta_mid, 2 * LANES), F32),
            pltpu.VMEM((dirs, slots, 2, band, LANES), F32),
            pltpu.VMEM((subs * tops, 2, band, LANES), F32),
            pltpu.VMEM((tops, listed, 2 * band, LANES), F32),
            pltpu.VMEM((tops, 2, band, LANES), F32),
            dma((tops,)),
            dma((slots,)),
            dma,
            dma((dirs, slots)),
            dma((dirs, slots)),
            dma((hops, slots)),
            dma((hops, slots)),
            dma((hops, slots)),
            dma((hops, slots)),
            dma((2 * hops + 1, slots)),
            dma((2 * hops + 1, slots)),
            dma((dirs,)),
            dma((dirs,)),
        ],
        compiler_params=pltpu.CompilerParams(
            vmem_limit_bytes=48 * 2**20, collective_id=0, has_side_effects=True),
        name="rise",
    )(fine_octant, mid_oct, place, x, wf, af, wt, at, cf, sf, ct, st, w)

    result = pl.pallas_call(
        down_kernel,
        out_shape=jax.ShapeDtypeStruct((rows * 2, LANES), F32),
        in_specs=[SM, SM] + [VM] * 9,
        out_specs=VM,
        scratch_shapes=[
            pltpu.VMEM((mids * theta_mid, 2 * LANES), F32),
            pltpu.VMEM((mids * theta_mid, LANES), F32),
            pltpu.VMEM((pack, rows, LANES), F32),
        ],
        compiler_params=params,
        name="down",
    )(fine_octant, mid_oct, parent, wf.T, af.T, wt.T, at.T, cf, sf, ct, st)
    return result.reshape(boxes, per, 2, LANES).transpose(0, 2, 1, 3).reshape(boxes, 2, theta_fine * phi_fine)


def solution(mesh):
    in_specs = (
        P(("sub", "dir"), None, None),
        P(("sub", "dir")),
        P("sub"),
        P(),
        P(),
        P(),
        P(),
        P(),
        P(),
        P("sub", None),
        P("sub", None, None, "dir"),
    )
    out_specs = P(("sub", "dir"), None, None)
    return jax.shard_map(body, mesh=mesh, in_specs=in_specs, out_specs=out_specs, check_vma=False)
```

```python
import jax
import jax.numpy as jnp
from jax import lax
from jax.experimental import pallas as pl
from jax.experimental.pallas import tpu as pltpu
from jax.sharding import PartitionSpec as P

LANES = 128
MESH = pl.DeviceIdType.MESH
BF = jnp.bfloat16
F32 = jnp.float32


def split(x):
    hi = x.astype(BF)
    return hi, (x - hi.astype(F32)).astype(BF)


def mm(a, b):
    return jnp.dot(a, b, preferred_element_type=F32)


def wide_dot(x, w_hi, w_lo):
    hi, lo = split(x)
    return mm(hi, w_hi) + (mm(hi, w_lo) + mm(lo, w_hi))


def left3(a):
    hi, lo = split(a)
    return jnp.concatenate([hi, lo, hi], axis=1)


def right3(x):
    hi, lo = split(x)
    return jnp.concatenate([hi, hi, lo], axis=0)


def wide_dot_t(x, w_hi, w_lo):
    def mt(a, b):
        return lax.dot_general(a, b, (((1,), (1,)), ((), ())), preferred_element_type=F32)

    hi, lo = split(x)
    return mt(hi, w_hi) + (mt(hi, w_lo) + mt(lo, w_hi))


def twice(b):
    zero = jnp.zeros_like(b)
    return jnp.concatenate([jnp.concatenate([b, zero], axis=1), jnp.concatenate([zero, b], axis=1)], axis=0)


def banded_rows(af_ref, pack):
    per = af_ref.shape[0] // pack
    return jnp.concatenate([af_ref[pl.ds(a, per, stride=pack), :] for a in range(pack)], axis=0)


def chunk_of(rows):
    return min(rows, 512)


def up_kernel(fine_oct, mid_oct, partners, x_ref, wf_ref, af_ref, wt_ref, at_ref, cf_ref, sf_ref, ct_ref, st_ref,
              w_hbm, out_ref, y_ref, mid_ref, z_ref, banded_ref, p_ref, w_ref, o_ref,
              w_sem, own_sem, last_sem, a_send, a_recv, cw_send, cw_recv, ccw_send, ccw_recv,
              part_send, part_recv, r_send, r_recv):
    pack, step, _ = y_ref.shape
    theta_mid = cf_ref.shape[1]
    theta_fine = af_ref.shape[0]
    per = theta_fine // pack
    half = LANES // 2
    dirs, slots, _, band, _ = banded_ref.shape
    tops, listed = w_ref.shape[:2]
    subs = p_ref.shape[0] // tops
    chips = subs // 2
    wide = chips // 2
    hops = chips // 2

    me = lax.axis_index("sub")
    z = lax.axis_index("dir")
    core = lax.rem(me, 2)

    def flip(c):
        return jnp.where(c < wide, c, 3 * wide - 1 - c)

    ring = flip(me // 2)

    def at_ring(move):
        return 2 * flip(lax.rem(ring + move + chips, chips)) + core

    right, left = at_ring(1), at_ring(-1)
    partner = me + 1 - 2 * core

    barrier = pltpu.get_barrier_semaphore()
    for e in range(1, dirs):
        pl.semaphore_signal(barrier, inc=1, device_id=(me, lax.rem(z + e, dirs)), device_id_type=MESH)
    for s in (right, left, partner):
        pl.semaphore_signal(barrier, inc=1, device_id=(s, z), device_id_type=MESH)
    loads = []
    for t in range(tops):
        copy = pltpu.make_async_copy(w_hbm.at[t], w_ref.at[t], w_sem.at[t])
        copy.start()
        loads.append(copy)
    pl.semaphore_wait(barrier, dirs + 2)

    def push(src, dst, send, recv, device):
        return pltpu.make_async_remote_copy(
            src_ref=src, dst_ref=dst, send_sem=send, recv_sem=recv, device_id=device, device_id_type=MESH)

    def spread(q):
        dst = p_ref.at[me * tops + q * dirs + z]
        copies = []
        for e in range(1, dirs):
            d = lax.rem(z - e + dirs, dirs)
            copies.append(push(banded_ref.at[d, q], dst, a_send.at[e, q], a_recv.at[e, q], (me, d)))
        return copies, pltpu.make_async_copy(banded_ref.at[z, q], dst, own_sem.at[q])

    def start_spread(q):
        copies, own = spread(q)
        for copy in copies:
            copy.start()
        own.start()

    def piece(sub, i):
        return p_ref.at[pl.ds(sub * tops + i * dirs, dirs)]

    def own_copies(q):
        view = piece(me, q)
        return [
            push(view, view, cw_send.at[0, q], cw_recv.at[0, q], (right, z)),
            push(view, view, ccw_send.at[0, q], ccw_recv.at[0, q], (left, z)),
            push(view, view, part_send.at[0, q], part_recv.at[0, q], (partner, z)),
        ]

    def own_ship(q):
        copies, own = spread(q)
        for copy in copies:
            copy.wait_recv()
        own.wait()
        for copy in own_copies(q):
            copy.start()

    wf_hi, wf_lo = split(wf_ref[...])
    wt_hi, wt_lo = split(twice(wt_ref[...]))
    a_mid = left3(banded_rows(af_ref, pack).T)
    a_top = left3(at_ref[...].T)
    banded_ref[...] = jnp.zeros_like(banded_ref)

    @pl.loop(0, slots)
    def _(q):
        base = pl.multiple_of(q * step, 8)
        re = x_ref[pl.ds(2 * base, step, stride=2), :]
        im = x_ref[pl.ds(2 * base + 1, step, stride=2), :]
        y = wide_dot(jnp.concatenate([re, im], axis=1), wf_hi, wf_lo)
        for a in range(pack):
            y_ref[a] = y[:, a * LANES:(a + 1) * LANES]

        @pl.when(q > 0)
        def _():
            start_spread(q - 1)

        @pl.when(q > 1)
        def _():
            own_ship(q - 2)

        def box(b):
            start = pl.multiple_of(b * per, per)
            return jnp.concatenate([y_ref[a, pl.ds(start, per), :] for a in range(pack)], axis=0)

        def mid_step(m, carry):
            acc1 = jnp.zeros((theta_mid, LANES), F32)
            acc2 = jnp.zeros((theta_mid, LANES), F32)
            for i in range(0, 8, 2):
                b = m * 8 + i
                v = mm(a_mid, right3(jnp.concatenate([box(b), box(b + 1)], axis=1)))
                for side in range(2):
                    o = fine_oct[q * 64 + b + side]
                    part = v[:, side * LANES:(side + 1) * LANES]
                    acc1 += part * cf_ref[o]
                    acc2 += part * sf_ref[o]
            mid_ref[pl.ds(pl.multiple_of(m * theta_mid, theta_mid), theta_mid), :] = acc1 + pltpu.roll(acc2, half, 1)
            return carry

        lax.fori_loop(0, 8, mid_step, 0, unroll=2)
        z_ref[...] = wide_dot(mid_ref[...], wt_hi, wt_lo)

        def top_step(m, carry):
            o = mid_oct[(z * slots + q) * 8 + m]
            v = mm(a_top, right3(z_ref[pl.ds(pl.multiple_of(m * theta_mid, theta_mid), theta_mid), :]))
            for d in range(dirs):
                at = slice(d * band, (d + 1) * band)
                c, s = ct_ref[o, at, :], st_ref[o, at, :]
                re, im = v[at, :LANES], v[at, LANES:]
                banded_ref[d, q, 0] += re * c - im * s
                banded_ref[d, q, 1] += re * s + im * c
            return carry

        lax.fori_loop(0, 8, top_step, 0, unroll=2)

    if slots > 1:
        own_ship(slots - 2)
    start_spread(slots - 1)

    sent, handed = [], []

    def ship(view, send, recv, device, keep):
        copy = push(view, view, send, recv, device)
        copy.start()
        keep.append(copy)

    for turn in range(1, slots + hops):
        if turn == min(slots, 2):
            own_ship(slots - 1)
        for h in range(1, hops + 1):
            i = turn - h
            if not 0 <= i < slots:
                continue
            for way in range(2):
                forward = i < slots // 2 if way == 0 else i >= slots // 2
                if h == hops and not forward:
                    continue
                send, recv = (cw_send, cw_recv) if way == 0 else (ccw_send, ccw_recv)
                target = right if way == 0 else left
                view = piece(at_ring(-h if way == 0 else h), i)
                push(view, view, send.at[h - 1, i], recv.at[h - 1, i], (target, z)).wait_recv()
                if h + 1 < hops or (h + 1 == hops and forward):
                    ship(view, send.at[h, i], recv.at[h, i], (target, z), sent)
                slot = 2 * h - 1 + way
                ship(view, part_send.at[slot, i], part_recv.at[slot, i], (partner, z), handed)
    for q in range(slots):
        own_copies(q)[2].wait_recv()
    for copy in handed:
        copy.wait_recv()
    for copy in loads:
        copy.wait()

    def translate(t):
        def one(k, carry):
            re, im = carry
            n = partners[t, k]
            inside = lax.rem(n, tops)
            n = n - inside + lax.rem(inside, slots) * dirs + lax.div(inside, slots)
            wr = w_ref[t, k, pl.ds(0, band, stride=2), :]
            wi = w_ref[t, k, pl.ds(1, band, stride=2), :]
            vr, vi = p_ref[n, 0], p_ref[n, 1]
            return re + (vr * wr - vi * wi), im + (vr * wi + vi * wr)

        zero = jnp.zeros((band, LANES), F32)
        re, im = lax.fori_loop(0, listed, one, (zero, zero), unroll=4)
        o_ref[t, 0] = re
        o_ref[t, 1] = im

    returns = []
    waiting = None
    for e in range(1, dirs + 1):
        d = lax.rem(z + e, dirs)
        translate(d * slots)
        if waiting is not None:
            waiting.start()
            returns.append(waiting)
            waiting = None
        if slots > 1:
            def more(q, carry, d=d):
                translate(d * slots + q)
                return carry

            lax.fori_loop(1, slots, more, 0)
        if e < dirs:
            waiting = push(o_ref.at[pl.ds(d * slots, slots)], out_ref.at[z], r_send.at[e], r_recv.at[e], (me, d))
    for copy in returns:
        copy.wait()
    own = pltpu.make_async_copy(o_ref.at[pl.ds(z * slots, slots)], out_ref.at[z], last_sem)
    own.start()
    for q in range(slots):
        for copy in spread(q)[0] + own_copies(q):
            copy.wait_send()
    for copy in sent + handed:
        copy.wait_send()
    own.wait()


def down_kernel(fine_oct, mid_oct, r_ref, wf_ref, af_ref, wt_ref, at_ref, cf_ref, sf_ref, ct_ref, st_ref,
                out_ref, z_ref, mid_ref, y_ref):
    pack = y_ref.shape[0]
    rows = y_ref.shape[1]
    theta_mid = cf_ref.shape[1]
    theta_fine = af_ref.shape[0]
    per = theta_fine // pack
    mids = mid_ref.shape[0] // theta_mid
    dirs = r_ref.shape[0]
    first_mid = lax.axis_index("dir") * mids
    half = LANES // 2

    a_hi, a_lo = split(at_ref[...])
    a_top = jnp.concatenate(
        [jnp.concatenate([a_hi, a_hi], axis=1), jnp.concatenate([a_lo, a_lo], axis=1)], axis=0)

    def top_step(m, carry):
        q = m // 8
        o = mid_oct[first_mid + m]
        c, s = ct_ref[o], st_ref[o]
        re = jnp.concatenate([r_ref[d, q, 0] for d in range(dirs)], axis=0)
        im = jnp.concatenate([r_ref[d, q, 1] for d in range(dirs)], axis=0)
        hi, lo = split(jnp.concatenate([re * c + im * s, im * c - re * s], axis=1))
        z = mm(a_top, jnp.concatenate([hi, lo], axis=0))
        z_ref[pl.ds(pl.multiple_of(m * theta_mid, theta_mid), theta_mid), :] = z[:theta_mid] + z[theta_mid:]
        return carry

    lax.fori_loop(0, mids, top_step, 0, unroll=2)

    wt_hi, wt_lo = split(twice(wt_ref[...]))
    mid_rows = mids * theta_mid
    step2 = chunk_of(mid_rows)

    @pl.loop(0, mid_rows // step2)
    def _(i):
        base = pl.multiple_of(i * step2, 8)
        mid_ref[pl.ds(base, step2), :] = wide_dot_t(z_ref[pl.ds(base, step2), :], wt_hi, wt_lo)

    a_mid = left3(banded_rows(af_ref, pack))

    def mid_step(m, carry):
        v = mid_ref[pl.ds(pl.multiple_of(m * theta_mid, theta_mid), theta_mid), :]
        turned = pltpu.roll(v, half, 1)
        for i in range(0, 8, 2):
            b = m * 8 + i
            both = []
            for side in range(2):
                o = fine_oct[b + side]
                both.append(v * cf_ref[o] + turned * sf_ref[o])
            z = mm(a_mid, right3(jnp.concatenate(both, axis=1)))
            for side in range(2):
                start = pl.multiple_of((b + side) * per, per)
                for a in range(pack):
                    y_ref[a, pl.ds(start, per), :] = z[a * per:(a + 1) * per, side * LANES:(side + 1) * LANES]
        return carry

    lax.fori_loop(0, mids, mid_step, 0, unroll=2)

    wf_hi, wf_lo = split(wf_ref[...])
    step = chunk_of(rows)

    @pl.loop(0, rows // step)
    def _(i):
        base = pl.multiple_of(i * step, 8)
        v = jnp.concatenate([y_ref[a, pl.ds(base, step), :] for a in range(pack)], axis=1)
        y = wide_dot(v, wf_hi, wf_lo)
        out_ref[pl.ds(2 * base, step, stride=2), :] = y[:, :LANES]
        out_ref[pl.ds(2 * base + 1, step, stride=2), :] = y[:, LANES:]


VM = pl.BlockSpec(memory_space=pltpu.VMEM)
SM = pl.BlockSpec(memory_space=pltpu.SMEM)
ANY = pl.BlockSpec(memory_space=pl.ANY)


def body(fine_fields, fine_octant, mid_octant, shift_fine, shift_mid, interp_theta_mid, interp_phi_mid,
         interp_theta_top, interp_phi_top, partners, translation):
    theta_mid, theta_fine = interp_theta_mid.shape
    phi_mid, phi_fine = interp_phi_mid.shape
    theta_top, _ = interp_theta_top.shape
    phi_top, _ = interp_phi_top.shape
    dirs = lax.axis_size("dir")
    boxes = fine_fields.shape[0]
    mids = boxes // 8
    slots = mids // 8
    tops, listed, _, local = translation.shape
    band = local // phi_top
    pack = LANES // phi_fine
    per = theta_fine // pack
    rows = boxes * per

    x = fine_fields.reshape(boxes, 2, per, LANES).transpose(0, 2, 1, 3).reshape(rows * 2, LANES)
    w = translation.reshape(tops, listed, 2, band, LANES).transpose(0, 1, 3, 2, 4).reshape(
        tops, listed, 2 * band, LANES)

    cos_f = jnp.cos(shift_fine).reshape(8, theta_mid, phi_mid)
    sin_f = jnp.sin(shift_fine).reshape(8, theta_mid, phi_mid)
    cf = jnp.concatenate([cos_f, cos_f], axis=2)
    sf = jnp.concatenate([sin_f, -sin_f], axis=2)
    ct = jnp.cos(shift_mid).reshape(8, theta_top, phi_top)
    st = jnp.sin(shift_mid).reshape(8, theta_top, phi_top)

    two = jnp.eye(2, dtype=F32)
    lots = jnp.eye(pack, dtype=F32)
    wf = (two[:, None, None, None, :, None] * lots[None, :, None, :, None, None]
          * interp_phi_mid.T[None, None, :, None, None, :]).reshape(2 * LANES, pack * 2 * phi_mid)
    af, wt, at = interp_theta_mid.T, interp_phi_top.T, interp_theta_top.T

    params = pltpu.CompilerParams(vmem_limit_bytes=48 * 2**20)
    subs = lax.axis_size("sub")
    hops = subs // 4
    dma = pltpu.SemaphoreType.DMA
    parent = pl.pallas_call(
        up_kernel,
        out_shape=jax.ShapeDtypeStruct((dirs, slots, 2, band, LANES), F32),
        in_specs=[SM] * 3 + [VM] * 9 + [ANY],
        out_specs=ANY,
        scratch_shapes=[
            pltpu.VMEM((pack, rows // slots, LANES), F32),
            pltpu.VMEM((8 * theta_mid, LANES), F32),
            pltpu.VMEM((8 * theta_mid, 2 * LANES), F32),
            pltpu.VMEM((dirs, slots, 2, band, LANES), F32),
            pltpu.VMEM((subs * tops, 2, band, LANES), F32),
            pltpu.VMEM((tops, listed, 2 * band, LANES), F32),
            pltpu.VMEM((tops, 2, band, LANES), F32),
            dma((tops,)),
            dma((slots,)),
            dma,
            dma((dirs, slots)),
            dma((dirs, slots)),
            dma((hops, slots)),
            dma((hops, slots)),
            dma((hops, slots)),
            dma((hops, slots)),
            dma((2 * hops + 1, slots)),
            dma((2 * hops + 1, slots)),
            dma((dirs,)),
            dma((dirs,)),
        ],
        compiler_params=pltpu.CompilerParams(
            vmem_limit_bytes=48 * 2**20, collective_id=0, has_side_effects=True),
        name="rise",
    )(fine_octant, mid_octant, partners, x, wf, af, wt, at, cf, sf, ct, st, w)

    result = pl.pallas_call(
        down_kernel,
        out_shape=jax.ShapeDtypeStruct((rows * 2, LANES), F32),
        in_specs=[SM, SM] + [VM] * 9,
        out_specs=VM,
        scratch_shapes=[
            pltpu.VMEM((mids * theta_mid, 2 * LANES), F32),
            pltpu.VMEM((mids * theta_mid, LANES), F32),
            pltpu.VMEM((pack, rows, LANES), F32),
        ],
        compiler_params=params,
        name="down",
    )(fine_octant, mid_octant, parent, wf.T, af, wt, at, cf, sf, ct, st)
    return result.reshape(boxes, per, 2, LANES).transpose(0, 2, 1, 3).reshape(boxes, 2, theta_fine * phi_fine)


def solution(mesh):
    in_specs = (
        P(("sub", "dir"), None, None),
        P(("sub", "dir")),
        P("sub"),
        P(),
        P(),
        P(),
        P(),
        P(),
        P(),
        P("sub", None),
        P("sub", None, None, "dir"),
    )
    out_specs = P(("sub", "dir"), None, None)
    return jax.shard_map(body, mesh=mesh, in_specs=in_specs, out_specs=out_specs, check_vma=False)
```

```python
import jax
import jax.numpy as jnp
from jax import lax
from jax.experimental import pallas as pl
from jax.experimental.pallas import tpu as pltpu
from jax.sharding import PartitionSpec as P

LANES = 128
MESH = pl.DeviceIdType.MESH
BF = jnp.bfloat16
F32 = jnp.float32


def split(x):
    hi = x.astype(BF)
    return hi, (x - hi.astype(F32)).astype(BF)


def mm(a, b):
    return jnp.dot(a, b, preferred_element_type=F32)


def wide_dot(x, w_hi, w_lo):
    hi, lo = split(x)
    return mm(hi, w_hi) + (mm(hi, w_lo) + mm(lo, w_hi))


def left3(a):
    hi, lo = split(a)
    return jnp.concatenate([hi, lo, hi], axis=1)


def right3(x):
    hi, lo = split(x)
    return jnp.concatenate([hi, hi, lo], axis=0)


def wide_dot_t(x, w_hi, w_lo):
    def mt(a, b):
        return lax.dot_general(a, b, (((1,), (1,)), ((), ())), preferred_element_type=F32)

    hi, lo = split(x)
    return mt(hi, w_hi) + (mt(hi, w_lo) + mt(lo, w_hi))


def twice(b):
    zero = jnp.zeros_like(b)
    return jnp.concatenate([jnp.concatenate([b, zero], axis=1), jnp.concatenate([zero, b], axis=1)], axis=0)


def banded_rows(af_ref, pack):
    per = af_ref.shape[0] // pack
    return jnp.concatenate([af_ref[pl.ds(a, per, stride=pack), :] for a in range(pack)], axis=0)


def chunk_of(rows):
    return min(rows, 512)


def up_kernel(fine_oct, mid_oct, partners, x_ref, wf_ref, af_ref, wt_ref, at_ref, cf_ref, sf_ref, ct_ref, st_ref,
              w_hbm, out_ref, y_ref, mid_ref, z_ref, banded_ref, p_ref, w_ref, o_ref,
              w_sem, own_sem, last_sem, a_send, a_recv, cw_send, cw_recv, ccw_send, ccw_recv,
              part_send, part_recv, r_send, r_recv):
    pack, step, _ = y_ref.shape
    theta_mid = cf_ref.shape[1]
    theta_fine = af_ref.shape[0]
    per = theta_fine // pack
    half = LANES // 2
    dirs, slots, _, band, _ = banded_ref.shape
    tops, listed = w_ref.shape[:2]
    subs = p_ref.shape[0] // tops
    chips = subs // 2
    wide = chips // 2
    hops = chips // 2

    me = lax.axis_index("sub")
    z = lax.axis_index("dir")
    core = lax.rem(me, 2)

    def flip(c):
        return jnp.where(c < wide, c, 3 * wide - 1 - c)

    ring = flip(me // 2)

    def at_ring(move):
        return 2 * flip(lax.rem(ring + move + chips, chips)) + core

    right, left = at_ring(1), at_ring(-1)
    partner = me + 1 - 2 * core

    barrier = pltpu.get_barrier_semaphore()
    for e in range(1, dirs):
        pl.semaphore_signal(barrier, inc=1, device_id=(me, lax.rem(z + e, dirs)), device_id_type=MESH)
    for s in (right, left, partner):
        pl.semaphore_signal(barrier, inc=1, device_id=(s, z), device_id_type=MESH)
    loads = []
    for t in range(tops):
        copy = pltpu.make_async_copy(w_hbm.at[t], w_ref.at[t], w_sem.at[t])
        copy.start()
        loads.append(copy)
    pl.semaphore_wait(barrier, dirs + 2)

    def push(src, dst, send, recv, device):
        return pltpu.make_async_remote_copy(
            src_ref=src, dst_ref=dst, send_sem=send, recv_sem=recv, device_id=device, device_id_type=MESH)

    def spread(q):
        dst = p_ref.at[me * tops + q * dirs + z]
        copies = []
        for e in range(1, dirs):
            d = lax.rem(z - e + dirs, dirs)
            copies.append(push(banded_ref.at[d, q], dst, a_send.at[e, q], a_recv.at[e, q], (me, d)))
        return copies, pltpu.make_async_copy(banded_ref.at[z, q], dst, own_sem.at[q])

    def start_spread(q):
        copies, own = spread(q)
        for copy in copies:
            copy.start()
        own.start()

    def piece(sub, i):
        return p_ref.at[pl.ds(sub * tops + i * dirs, dirs)]

    def own_copies(q):
        view = piece(me, q)
        return [
            push(view, view, cw_send.at[0, q], cw_recv.at[0, q], (right, z)),
            push(view, view, ccw_send.at[0, q], ccw_recv.at[0, q], (left, z)),
            push(view, view, part_send.at[0, q], part_recv.at[0, q], (partner, z)),
        ]

    def own_ship(q):
        copies, own = spread(q)
        for copy in copies:
            copy.wait_recv()
        own.wait()
        for copy in own_copies(q):
            copy.start()

    wf_hi, wf_lo = split(wf_ref[...])
    wt_hi, wt_lo = split(twice(wt_ref[...]))
    a_mid = left3(banded_rows(af_ref, pack).T)
    a_top = left3(at_ref[...].T)
    banded_ref[...] = jnp.zeros_like(banded_ref)

    @pl.loop(0, slots)
    def _(q):
        base = pl.multiple_of(q * step, 8)
        re = x_ref[pl.ds(2 * base, step, stride=2), :]
        im = x_ref[pl.ds(2 * base + 1, step, stride=2), :]
        y = wide_dot(jnp.concatenate([re, im], axis=1), wf_hi, wf_lo)
        for a in range(pack):
            y_ref[a] = y[:, a * LANES:(a + 1) * LANES]

        @pl.when(q > 0)
        def _():
            start_spread(q - 1)

        @pl.when(q > 1)
        def _():
            own_ship(q - 2)

        def box(b):
            start = pl.multiple_of(b * per, per)
            return jnp.concatenate([y_ref[a, pl.ds(start, per), :] for a in range(pack)], axis=0)

        def mid_step(m, carry):
            acc1 = jnp.zeros((theta_mid, LANES), F32)
            acc2 = jnp.zeros((theta_mid, LANES), F32)
            for i in range(0, 8, 2):
                b = m * 8 + i
                v = mm(a_mid, right3(jnp.concatenate([box(b), box(b + 1)], axis=1)))
                for side in range(2):
                    o = fine_oct[q * 64 + b + side]
                    part = v[:, side * LANES:(side + 1) * LANES]
                    acc1 += part * cf_ref[o]
                    acc2 += part * sf_ref[o]
            mid_ref[pl.ds(pl.multiple_of(m * theta_mid, theta_mid), theta_mid), :] = acc1 + pltpu.roll(acc2, half, 1)
            return carry

        lax.fori_loop(0, 8, mid_step, 0, unroll=4)
        z_ref[...] = wide_dot(mid_ref[...], wt_hi, wt_lo)

        def top_step(m, carry):
            o = mid_oct[(z * slots + q) * 8 + m]
            v = mm(a_top, right3(z_ref[pl.ds(pl.multiple_of(m * theta_mid, theta_mid), theta_mid), :]))
            for d in range(dirs):
                at = slice(d * band, (d + 1) * band)
                c, s = ct_ref[o, at, :], st_ref[o, at, :]
                re, im = v[at, :LANES], v[at, LANES:]
                banded_ref[d, q, 0] += re * c - im * s
                banded_ref[d, q, 1] += re * s + im * c
            return carry

        lax.fori_loop(0, 8, top_step, 0, unroll=4)

    if slots > 1:
        own_ship(slots - 2)
    start_spread(slots - 1)

    sent, handed = [], []

    def ship(view, send, recv, device, keep):
        copy = push(view, view, send, recv, device)
        copy.start()
        keep.append(copy)

    for turn in range(1, slots + hops):
        if turn == min(slots, 2):
            own_ship(slots - 1)
        for h in range(1, hops + 1):
            i = turn - h
            if not 0 <= i < slots:
                continue
            for way in range(2):
                forward = i < slots // 2 if way == 0 else i >= slots // 2
                if h == hops and not forward:
                    continue
                send, recv = (cw_send, cw_recv) if way == 0 else (ccw_send, ccw_recv)
                target = right if way == 0 else left
                view = piece(at_ring(-h if way == 0 else h), i)
                push(view, view, send.at[h - 1, i], recv.at[h - 1, i], (target, z)).wait_recv()
                if h + 1 < hops or (h + 1 == hops and forward):
                    ship(view, send.at[h, i], recv.at[h, i], (target, z), sent)
                slot = 2 * h - 1 + way
                ship(view, part_send.at[slot, i], part_recv.at[slot, i], (partner, z), handed)
    for q in range(slots):
        own_copies(q)[2].wait_recv()
    for copy in handed:
        copy.wait_recv()
    for copy in loads:
        copy.wait()

    def translate(t):
        def one(k, carry):
            re, im = carry
            n = partners[t, k]
            inside = lax.rem(n, tops)
            n = n - inside + lax.rem(inside, slots) * dirs + lax.div(inside, slots)
            wr = w_ref[t, k, pl.ds(0, band, stride=2), :]
            wi = w_ref[t, k, pl.ds(1, band, stride=2), :]
            vr, vi = p_ref[n, 0], p_ref[n, 1]
            return re + (vr * wr - vi * wi), im + (vr * wi + vi * wr)

        zero = jnp.zeros((band, LANES), F32)
        re, im = lax.fori_loop(0, listed, one, (zero, zero), unroll=4)
        o_ref[t, 0] = re
        o_ref[t, 1] = im

    returns = []
    waiting = None
    for e in range(1, dirs + 1):
        d = lax.rem(z + e, dirs)
        translate(d * slots)
        if waiting is not None:
            waiting.start()
            returns.append(waiting)
            waiting = None
        if slots > 1:
            def more(q, carry, d=d):
                translate(d * slots + q)
                return carry

            lax.fori_loop(1, slots, more, 0)
        if e < dirs:
            waiting = push(o_ref.at[pl.ds(d * slots, slots)], out_ref.at[z], r_send.at[e], r_recv.at[e], (me, d))
    for copy in returns:
        copy.wait()
    own = pltpu.make_async_copy(o_ref.at[pl.ds(z * slots, slots)], out_ref.at[z], last_sem)
    own.start()
    for q in range(slots):
        for copy in spread(q)[0] + own_copies(q):
            copy.wait_send()
    for copy in sent + handed:
        copy.wait_send()
    own.wait()


def down_kernel(fine_oct, mid_oct, r_ref, wf_ref, af_ref, wt_ref, at_ref, cf_ref, sf_ref, ct_ref, st_ref,
                out_ref, z_ref, mid_ref, y_ref):
    pack = y_ref.shape[0]
    rows = y_ref.shape[1]
    theta_mid = cf_ref.shape[1]
    theta_fine = af_ref.shape[0]
    per = theta_fine // pack
    mids = mid_ref.shape[0] // theta_mid
    dirs = r_ref.shape[0]
    first_mid = lax.axis_index("dir") * mids
    half = LANES // 2

    a_hi, a_lo = split(at_ref[...])
    a_top = jnp.concatenate(
        [jnp.concatenate([a_hi, a_hi], axis=1), jnp.concatenate([a_lo, a_lo], axis=1)], axis=0)

    def top_step(m, carry):
        q = m // 8
        o = mid_oct[first_mid + m]
        c, s = ct_ref[o], st_ref[o]
        re = jnp.concatenate([r_ref[d, q, 0] for d in range(dirs)], axis=0)
        im = jnp.concatenate([r_ref[d, q, 1] for d in range(dirs)], axis=0)
        hi, lo = split(jnp.concatenate([re * c + im * s, im * c - re * s], axis=1))
        z = mm(a_top, jnp.concatenate([hi, lo], axis=0))
        z_ref[pl.ds(pl.multiple_of(m * theta_mid, theta_mid), theta_mid), :] = z[:theta_mid] + z[theta_mid:]
        return carry

    lax.fori_loop(0, mids, top_step, 0, unroll=4)

    wt_hi, wt_lo = split(twice(wt_ref[...]))
    mid_rows = mids * theta_mid
    step2 = chunk_of(mid_rows)

    @pl.loop(0, mid_rows // step2)
    def _(i):
        base = pl.multiple_of(i * step2, 8)
        mid_ref[pl.ds(base, step2), :] = wide_dot_t(z_ref[pl.ds(base, step2), :], wt_hi, wt_lo)

    a_mid = left3(banded_rows(af_ref, pack))

    def mid_step(m, carry):
        v = mid_ref[pl.ds(pl.multiple_of(m * theta_mid, theta_mid), theta_mid), :]
        turned = pltpu.roll(v, half, 1)
        for i in range(0, 8, 2):
            b = m * 8 + i
            both = []
            for side in range(2):
                o = fine_oct[b + side]
                both.append(v * cf_ref[o] + turned * sf_ref[o])
            z = mm(a_mid, right3(jnp.concatenate(both, axis=1)))
            for side in range(2):
                start = pl.multiple_of((b + side) * per, per)
                for a in range(pack):
                    y_ref[a, pl.ds(start, per), :] = z[a * per:(a + 1) * per, side * LANES:(side + 1) * LANES]
        return carry

    lax.fori_loop(0, mids, mid_step, 0, unroll=4)

    wf_hi, wf_lo = split(wf_ref[...])
    step = chunk_of(rows)

    @pl.loop(0, rows // step)
    def _(i):
        base = pl.multiple_of(i * step, 8)
        v = jnp.concatenate([y_ref[a, pl.ds(base, step), :] for a in range(pack)], axis=1)
        y = wide_dot(v, wf_hi, wf_lo)
        out_ref[pl.ds(2 * base, step, stride=2), :] = y[:, :LANES]
        out_ref[pl.ds(2 * base + 1, step, stride=2), :] = y[:, LANES:]


VM = pl.BlockSpec(memory_space=pltpu.VMEM)
SM = pl.BlockSpec(memory_space=pltpu.SMEM)
ANY = pl.BlockSpec(memory_space=pl.ANY)


def body(fine_fields, fine_octant, mid_octant, shift_fine, shift_mid, interp_theta_mid, interp_phi_mid,
         interp_theta_top, interp_phi_top, partners, translation):
    theta_mid, theta_fine = interp_theta_mid.shape
    phi_mid, phi_fine = interp_phi_mid.shape
    theta_top, _ = interp_theta_top.shape
    phi_top, _ = interp_phi_top.shape
    dirs = lax.axis_size("dir")
    boxes = fine_fields.shape[0]
    mids = boxes // 8
    slots = mids // 8
    tops, listed, _, local = translation.shape
    band = local // phi_top
    pack = LANES // phi_fine
    per = theta_fine // pack
    rows = boxes * per

    x = fine_fields.reshape(boxes, 2, per, LANES).transpose(0, 2, 1, 3).reshape(rows * 2, LANES)
    w = translation.reshape(tops, listed, 2, band, LANES).transpose(0, 1, 3, 2, 4).reshape(
        tops, listed, 2 * band, LANES)

    cos_f = jnp.cos(shift_fine).reshape(8, theta_mid, phi_mid)
    sin_f = jnp.sin(shift_fine).reshape(8, theta_mid, phi_mid)
    cf = jnp.concatenate([cos_f, cos_f], axis=2)
    sf = jnp.concatenate([sin_f, -sin_f], axis=2)
    ct = jnp.cos(shift_mid).reshape(8, theta_top, phi_top)
    st = jnp.sin(shift_mid).reshape(8, theta_top, phi_top)

    two = jnp.eye(2, dtype=F32)
    lots = jnp.eye(pack, dtype=F32)
    wf = (two[:, None, None, None, :, None] * lots[None, :, None, :, None, None]
          * interp_phi_mid.T[None, None, :, None, None, :]).reshape(2 * LANES, pack * 2 * phi_mid)
    af, wt, at = interp_theta_mid.T, interp_phi_top.T, interp_theta_top.T

    params = pltpu.CompilerParams(vmem_limit_bytes=48 * 2**20)
    subs = lax.axis_size("sub")
    hops = subs // 4
    dma = pltpu.SemaphoreType.DMA
    parent = pl.pallas_call(
        up_kernel,
        out_shape=jax.ShapeDtypeStruct((dirs, slots, 2, band, LANES), F32),
        in_specs=[SM] * 3 + [VM] * 9 + [ANY],
        out_specs=ANY,
        scratch_shapes=[
            pltpu.VMEM((pack, rows // slots, LANES), F32),
            pltpu.VMEM((8 * theta_mid, LANES), F32),
            pltpu.VMEM((8 * theta_mid, 2 * LANES), F32),
            pltpu.VMEM((dirs, slots, 2, band, LANES), F32),
            pltpu.VMEM((subs * tops, 2, band, LANES), F32),
            pltpu.VMEM((tops, listed, 2 * band, LANES), F32),
            pltpu.VMEM((tops, 2, band, LANES), F32),
            dma((tops,)),
            dma((slots,)),
            dma,
            dma((dirs, slots)),
            dma((dirs, slots)),
            dma((hops, slots)),
            dma((hops, slots)),
            dma((hops, slots)),
            dma((hops, slots)),
            dma((2 * hops + 1, slots)),
            dma((2 * hops + 1, slots)),
            dma((dirs,)),
            dma((dirs,)),
        ],
        compiler_params=pltpu.CompilerParams(
            vmem_limit_bytes=48 * 2**20, collective_id=0, has_side_effects=True),
        name="rise",
    )(fine_octant, mid_octant, partners, x, wf, af, wt, at, cf, sf, ct, st, w)

    result = pl.pallas_call(
        down_kernel,
        out_shape=jax.ShapeDtypeStruct((rows * 2, LANES), F32),
        in_specs=[SM, SM] + [VM] * 9,
        out_specs=VM,
        scratch_shapes=[
            pltpu.VMEM((mids * theta_mid, 2 * LANES), F32),
            pltpu.VMEM((mids * theta_mid, LANES), F32),
            pltpu.VMEM((pack, rows, LANES), F32),
        ],
        compiler_params=params,
        name="down",
    )(fine_octant, mid_octant, parent, wf.T, af, wt, at, cf, sf, ct, st)
    return result.reshape(boxes, per, 2, LANES).transpose(0, 2, 1, 3).reshape(boxes, 2, theta_fine * phi_fine)


def solution(mesh):
    in_specs = (
        P(("sub", "dir"), None, None),
        P(("sub", "dir")),
        P("sub"),
        P(),
        P(),
        P(),
        P(),
        P(),
        P(),
        P("sub", None),
        P("sub", None, None, "dir"),
    )
    out_specs = P(("sub", "dir"), None, None)
    return jax.shard_map(body, mesh=mesh, in_specs=in_specs, out_specs=out_specs, check_vma=False)
```
